128 devices in a mesh: seq: 8 (over x_lo, y), mp: 16 (over z, x_hi, core).
Axes of the slice: x: 4 (x_hi: 2, x_lo: 2; x = x_hi * 2 + x_lo), y: 4, z: 4, core: 2. Of those that a mesh axis runs over, the one named last changes fastest.
Arguments:
- audio_feats: bfloat16 [65536, 512], P(('seq', 'mp')), may hold values from -6 to 6
- conv_first: bfloat16 [3, 3, 512, 256], replicated, may hold values from -0.15625 to 0.15625
- conv_second: bfloat16 [3, 256, 512], replicated, may hold values from -0.375 to 0.375
- down_weight: bfloat16 [16, 512, 512], replicated, may hold values from -0.09375 to 0.09375
- in_proj: bfloat16 [512, 4096], replicated, may hold values from -0.25 to 0.25
- norm_gain: float32 [4096], replicated, may hold values from 0.25 to 1.75
- qkv_weight: bfloat16 [3, 4096, 2048], P(None, None, 'mp'), may hold values from -0.09375 to 0.09375
- out_weight: bfloat16 [2048, 4096], P('mp'), may hold values from -0.125 to 0.125
Outputs:
- layer_out: bfloat16 [8192, 4096], P(('seq', 'mp'))
The draws below stay inside these ranges and needn't reach their ends.
All inputs are finite; a program needn't handle non-finite values.
Results may differ from the reference program's by a relative error of at most 0.023.
Values may be sent and summed in bfloat16 or wider, within the bound.
No kernel may reach another device: no remote copies, remote signals or barrier semaphores. Data moves between devices by JAX's collectives and lax.ppermute only.
A program may use at most 128 MiB of HBM per device.

```python
import jax
import jax.numpy as jnp
from jax import lax

D = 4096
HEADS = 16
HD = 128
INNER = 2048
CH = 512
HALF = 256
STRIDE = 8
KSIZE = 16
STEPS = 65536
N_MP = 16


def draw_qkv_weight(key, part):
    inner = HEADS * HD
    scale = D ** (-0.5)
    keys = jax.random.split(key, 1)
    return (jnp.clip(jax.random.normal(keys[0], (3, D, inner), jnp.float32), -6.0, 6.0) * scale).astype(jnp.bfloat16)


def block_scale(key, extent, cuts, least, high):
    factor_of = 1.0
    for position, shards_of in cuts:
        steps = jax.random.uniform(jax.random.fold_in(jax.random.fold_in(key, 6), position), (shards_of,), jnp.float32, least / len(cuts), high / len(cuts))
        factor_of = factor_of * jnp.repeat(jnp.exp(steps), extent[position] // shards_of).reshape((-1,) + (1,) * (len(extent) - 1 - position))
    return factor_of


def noise(stream_key, extent, spread, limit, pieces=(), held_as=jnp.bfloat16):
    values = spread * jax.random.normal(stream_key, extent, jnp.float32)
    if pieces:
        values = values * block_scale(stream_key, extent, pieces, -0.22, 0.18)
    return jnp.clip(values, -limit, limit).astype(held_as)


def setup_inputs(seed: int = 0) -> dict:
    streams_of = jax.random.split(jax.random.key(seed), 9)
    return {
        "audio_feats": noise(streams_of[0], (STEPS, CH), 1.0, 6.0, ((0, 128),)),
        "conv_first": noise(streams_of[1], (3, 3, CH, HALF), (3 * CH) ** -0.5, 0.15625),
        "conv_second": noise(streams_of[2], (3, HALF, CH), HALF ** -0.5, 0.375),
        "down_weight": noise(streams_of[3], (KSIZE, CH, CH), (KSIZE * CH // 2) ** -0.5, 0.09375),
        "in_proj": noise(streams_of[4], (CH, D), CH ** -0.5, 0.25),
        "norm_gain": jnp.clip(1.0 + 0.15 * jax.random.normal(streams_of[5], (D,), jnp.float32), 0.25, 1.75),
        "qkv_weight": draw_qkv_weight(jax.random.fold_in(streams_of[8], 71), 0),
        "out_weight": noise(streams_of[7], (INNER, D), INNER ** -0.5, 0.125, ((0, 16),)),
    }


def causal_conv(u, weights, dilation):
    count = u.shape[0]
    padded = jnp.pad(u, ((2 * dilation, 0), (0, 0)))
    total = jnp.dot(padded[0:count], weights[0], preferred_element_type=jnp.float32)
    total = total + jnp.dot(padded[dilation:dilation + count], weights[1], preferred_element_type=jnp.float32)
    total = total + jnp.dot(padded[2 * dilation:2 * dilation + count], weights[2], preferred_element_type=jnp.float32)
    return total

def residual_unit(state, first, second, dilation):
    act = jax.nn.elu(state.astype(jnp.float32)).astype(jnp.bfloat16)
    middle = causal_conv(act, first, dilation)
    inner = jax.nn.elu(middle).astype(jnp.bfloat16)
    return (state.astype(jnp.float32) + jnp.dot(inner, second, preferred_element_type=jnp.float32)).astype(jnp.bfloat16)

def attend_heads(heads_q, heads_k, heads_v):
    length = heads_q.shape[1]
    qblock = min(1024, length)
    scale = HD ** (-0.5)
    results = []
    for block in range(length // qblock):
        begin = block * qblock
        stop = begin + qblock
        qpos = begin + jnp.arange(qblock, dtype=jnp.int32)
        kpos = jnp.arange(stop, dtype=jnp.int32)
        mask = kpos[None, :] <= qpos[:, None]

        def one(trio):
            scores = jnp.dot(trio[0][begin:stop], trio[1][:stop].T, preferred_element_type=jnp.float32) * scale
            scores = jnp.where(mask, scores, -1e+30)
            peak = lax.optimization_barrier(jnp.max(scores, axis=1, keepdims=True))
            probs = jnp.where(mask, jnp.exp(scores - peak), 0.0)
            total = lax.optimization_barrier(jnp.sum(probs, axis=1, keepdims=True))
            mixed = jnp.dot(probs.astype(jnp.bfloat16), trio[2][:stop], preferred_element_type=jnp.float32)
            return mixed / total
        results.append(lax.map(one, (heads_q, heads_k, heads_v)))
    return jnp.concatenate(results, axis=1)

def reference(audio_feats, conv_first, conv_second, down_weight, in_proj, norm_gain, qkv_weight, out_weight):
    state = audio_feats
    for unit, dilation in enumerate((1, 3, 9)):
        state = residual_unit(state, conv_first[unit], conv_second[unit], dilation)
    act = jax.nn.elu(state.astype(jnp.float32)).astype(jnp.bfloat16)
    padded = jnp.pad(act, ((STRIDE, 0), (0, 0)))
    channels = act.shape[1]
    grouped = padded.reshape(-1, STRIDE * channels)
    taps = down_weight.reshape(2, STRIDE * channels, channels)
    latent = (jnp.dot(grouped[:-1], taps[0], preferred_element_type=jnp.float32) + jnp.dot(grouped[1:], taps[1], preferred_element_type=jnp.float32)).astype(jnp.bfloat16)
    frames = jnp.dot(latent, in_proj, preferred_element_type=jnp.float32).astype(jnp.bfloat16)
    wide = frames.astype(jnp.float32)
    normed = (wide * lax.rsqrt(lax.optimization_barrier(jnp.mean(wide * wide, axis=1, keepdims=True)) + 1e-05) * norm_gain).astype(jnp.bfloat16)
    query = jnp.dot(normed, qkv_weight[0], preferred_element_type=jnp.float32).astype(jnp.bfloat16)
    keys = jnp.dot(normed, qkv_weight[1], preferred_element_type=jnp.float32).astype(jnp.bfloat16)
    values = jnp.dot(normed, qkv_weight[2], preferred_element_type=jnp.float32).astype(jnp.bfloat16)
    length = query.shape[0]
    heads_q = query.reshape(length, HEADS, HD).transpose(1, 0, 2)
    heads_k = keys.reshape(length, HEADS, HD).transpose(1, 0, 2)
    heads_v = values.reshape(length, HEADS, HD).transpose(1, 0, 2)
    mixed = attend_heads(heads_q, heads_k, heads_v)
    attn = mixed.transpose(1, 0, 2).reshape(length, HEADS * HD).astype(jnp.bfloat16)
    group_width = attn.shape[1] // N_MP
    attn_groups = attn.reshape(length, N_MP, group_width).transpose(1, 0, 2)
    weight_groups = out_weight.reshape(N_MP, group_width, out_weight.shape[1])

    def add_group(total, pair):
        part = jnp.dot(pair[0], pair[1], preferred_element_type=jnp.float32)
        rounded = lax.optimization_barrier(part.astype(jnp.bfloat16))
        return (total + rounded.astype(jnp.float32), None)
    summed, _ = lax.scan(add_group, jnp.zeros((length, out_weight.shape[1]), jnp.float32), (attn_groups, weight_groups))
    return (wide + summed).astype(jnp.bfloat16)
```

```python
import jax
import jax.numpy as jnp
from jax import lax
from jax.experimental import pallas as pl
from jax.experimental.pallas import tpu as pltpu
from jax.sharding import PartitionSpec as P

HD = 128
HALO = 48
DILATIONS = (1, 3, 9)
AXES = ("seq", "mp")
F32 = jnp.float32
BF16 = jnp.bfloat16
QSCALE = 1.4426950408889634 * HD ** (-0.5)


def decode(i):
    s, m = divmod(i, 16)
    xl, y = divmod(s, 4)
    z, r = divmod(m, 4)
    xh, c = divmod(r, 2)
    return 2 * xh + xl, y, z, c


def encode(x, y, z, c):
    xh, xl = divmod(x % 4, 2)
    return (xl * 4 + y % 4) * 16 + (z % 4) * 4 + xh * 2 + c


def send(value, target):
    return lax.ppermute(value, AXES, [(i, encode(*target(*decode(i)))) for i in range(128)])


def swap_core(value):
    return send(value, lambda x, y, z, c: (x, y, z, 1 - c))


def from_x(value, d):
    return send(value, lambda x, y, z, c: (x - d, y, z, c))


def from_y(value, d):
    return send(value, lambda x, y, z, c: (x, y - d, z, c))


def from_z(value, d):
    return send(value, lambda x, y, z, c: (x, y, z - d, c))


def from_first(value, d):
    return send(value, lambda x, y, z, c: (x - d, y, z, c) if c == 0 else (x, y, z - d, c))


def from_second(value, d):
    return send(value, lambda x, y, z, c: (x, y, z - d, c) if c == 0 else (x - d, y, z, c))


def place():
    s = lax.axis_index("seq")
    m = lax.axis_index("mp")
    xl, y = s // 4, s % 4
    z, xh, c = m // 4, (m // 2) % 2, m % 2
    return 2 * xh + xl, y, z, c


def elu(v):
    return jnp.where(v > 0, v, jnp.tanh(0.5 * v) * (jnp.exp(jnp.minimum(v, 0.0)) + 1.0))


def dot(a, b):
    return lax.dot_general(a, b, (((1,), (0,)), ((), ())), preferred_element_type=F32)


VMEM_SPEC = pl.BlockSpec(memory_space=pltpu.VMEM)
ANY_SPEC = pl.BlockSpec(memory_space=pl.ANY)


def params():
    return pltpu.CompilerParams(vmem_limit_bytes=56 * 1024 * 1024)


def encoder_kernel(
    halo, audio, first_hbm, second_hbm, down_hbm, proj_hbm,
    frames, latent,
    first, second, down, proj, state, taps, act, sems,
):
    copies = [
        pltpu.make_async_copy(first_hbm, first, sems.at[0]),
        pltpu.make_async_copy(second_hbm, second, sems.at[1]),
        pltpu.make_async_copy(down_hbm, down, sems.at[2]),
        pltpu.make_async_copy(proj_hbm, proj, sems.at[3]),
    ]
    for copy in copies:
        copy.start()
    rows = audio.shape[0]
    total = HALO + rows
    pad = 24
    state[0:HALO, :] = halo[...].astype(F32)
    state[HALO:total, :] = audio[...].astype(F32)
    taps[:, 0:pad, :] = jnp.zeros((3, pad, taps.shape[2]), F32)
    for unit, d in enumerate(DILATIONS):
        u = elu(state[...]).astype(BF16)
        if unit == 0:
            copies[0].wait()
            copies[1].wait()
        for k in range(3):
            taps[k, pad:pad + total, :] = dot(u, first[unit, k])
        middle = taps[0, pad - 2 * d:pad - 2 * d + total, :]
        middle = middle + taps[1, pad - d:pad - d + total, :]
        middle = middle + taps[2, pad:pad + total, :]
        v = elu(middle).astype(BF16)
        fresh = state[...] + dot(v, second[unit])
        state[...] = fresh.astype(BF16).astype(F32)
    lanes = act.shape[2]
    for j in range(act.shape[0]):
        act[j] = elu(state[:, j * lanes:(j + 1) * lanes]).astype(BF16).astype(F32)
    copies[2].wait()
    count = rows // 8
    mixed = jnp.zeros((count, down.shape[2]), F32)
    for k in range(16):
        picked = jnp.concatenate(
            [act[j, pl.ds(HALO - 8 + k, count, stride=8), :] for j in range(act.shape[0])], axis=1
        ).astype(BF16)
        mixed = mixed + dot(picked, down[k])
    lat = mixed.astype(BF16)
    copies[3].wait()
    wide = dot(lat, proj[...]).astype(BF16)
    frames[...] = wide
    wide = wide.astype(F32)
    mean = jnp.mean(wide * wide, axis=1, keepdims=True)
    latent[...] = (lat.astype(F32) * lax.rsqrt(mean + 1e-05)).astype(BF16)


def encode_frames(halo, audio, first, second, down, proj):
    rows, ch = audio.shape
    half = first.shape[3]
    total = HALO + rows
    return pl.pallas_call(
        encoder_kernel,
        out_shape=(
            jax.ShapeDtypeStruct((rows // 8, proj.shape[1]), BF16),
            jax.ShapeDtypeStruct((rows // 8, ch), BF16),
        ),
        in_specs=[VMEM_SPEC, VMEM_SPEC, ANY_SPEC, ANY_SPEC, ANY_SPEC, ANY_SPEC],
        out_specs=(VMEM_SPEC, VMEM_SPEC),
        scratch_shapes=[
            pltpu.VMEM(first.shape, BF16),
            pltpu.VMEM(second.shape, BF16),
            pltpu.VMEM(down.shape, BF16),
            pltpu.VMEM(proj.shape, BF16),
            pltpu.VMEM((total, ch), F32),
            pltpu.VMEM((3, total + 24, half), F32),
            pltpu.VMEM((ch // 128, total, 128), F32),
            pltpu.SemaphoreType.DMA((4,)),
        ],
        compiler_params=params(),
        name="encoder",
    )(halo, audio, first, second, down, proj)


def compose_kernel(proj, gain, weight, out, acc):
    step = pl.program_id(0)

    @pl.when(step == 0)
    def _():
        acc[...] = jnp.zeros_like(acc)

    left = (proj[...].astype(F32) * gain[...]).astype(BF16)
    right = jnp.concatenate([weight[0], weight[1], weight[2]], axis=1)
    acc[...] += dot(left, right)

    @pl.when(step == pl.num_programs(0) - 1)
    def _():
        lanes = lax.broadcasted_iota(jnp.int32, acc.shape, 1)
        out[...] = (acc[...] * jnp.where(lanes < HD, QSCALE, 1.0)).astype(BF16)


def compose(proj, gain, weight):
    ch, width = proj.shape
    block = 1024
    return pl.pallas_call(
        compose_kernel,
        out_shape=jax.ShapeDtypeStruct((ch, 3 * HD), BF16),
        grid=(width // block,),
        in_specs=[
            pl.BlockSpec((ch, block), lambda i: (0, i)),
            pl.BlockSpec((1, block), lambda i: (0, i)),
            pl.BlockSpec((3, block, HD), lambda i: (0, i, 0)),
        ],
        out_specs=pl.BlockSpec((ch, 3 * HD), lambda i: (0, 0)),
        scratch_shapes=[pltpu.VMEM((ch, 3 * HD), F32)],
        compiler_params=params(),
        name="compose",
    )(proj, gain.reshape(1, width), weight)


def qkv_kernel(*refs):
    pieces, own, other = refs[0:8], refs[8], refs[9]
    query, pairs, mine, weight = refs[10:14]
    x, y, z, c = place()
    weight[...] = jnp.where(x % 2 == c, own[...], other[...])
    for side in range(2):
        core = c if side == 0 else 1 - c
        for far in range(4):
            got = dot(pieces[side * 4 + far][...], weight[...]).astype(BF16)
            for near in range(4):
                dx = jnp.where(core == 0, near, far)
                dz = jnp.where(core == 0, far, near)
                ox = (x + dx) % 4
                oz = (z + dz) % 4
                slot = oz * 2 + ox // 2
                part = got[near * 64:(near + 1) * 64, :]
                row = pl.multiple_of((ox % 2) * 1024 + slot * 128 + core * 64, 64)
                pairs[pl.ds(row, 64), :] = part[:, HD:]
                if side == 0:
                    row = pl.multiple_of((ox % 2) * 512 + slot * 64, 64)
                    query[pl.ds(row, 64), :] = part[:, :HD]
    mine[...] = pairs[pl.ds(pl.multiple_of(c * 1024, 1024), 1024), :]


def make_qkv(pieces, own, other):
    return pl.pallas_call(
        qkv_kernel,
        out_shape=(
            jax.ShapeDtypeStruct((1024, HD), BF16),
            jax.ShapeDtypeStruct((2048, 2 * HD), BF16),
            jax.ShapeDtypeStruct((1024, 2 * HD), BF16),
        ),
        in_specs=[VMEM_SPEC] * 10,
        out_specs=(VMEM_SPEC,) * 3,
        scratch_shapes=[pltpu.VMEM(own.shape, BF16)],
        compiler_params=params(),
        name="qkv",
    )(*pieces, own, other)


def absorb(query, keys, values, peak, total, accum, rows, mask=None):
    scores = lax.dot_general(query, keys, (((1,), (1,)), ((), ())), preferred_element_type=F32)
    if mask is not None:
        scores = jnp.where(mask, scores, -1e30)
    old = peak[rows, :]
    fresh = jnp.maximum(old, jnp.max(scores, axis=1, keepdims=True))
    probs = jnp.exp2(scores - fresh[:, :1])
    factor = jnp.exp2(old - fresh)
    total[rows, :] = total[rows, :] * factor + jnp.sum(probs, axis=1, keepdims=True)
    accum[rows, :] = accum[rows, :] * factor + dot(probs.astype(BF16), values)
    peak[rows, :] = fresh


def own_kernel(query, pairs, peak, total, accum):
    c = lax.axis_index("mp") % 2
    peak[...] = jnp.full(peak.shape, -1e30, F32)
    total[...] = jnp.zeros(total.shape, F32)
    accum[...] = jnp.zeros(accum.shape, F32)
    for block in range(2):
        for tile in range(4):
            rows = pl.ds(block * 512 + tile * 128, 128)
            q = query[rows, :]
            base = block * 1024
            r = lax.broadcasted_iota(jnp.int32, (128, 256), 0)
            k = lax.broadcasted_iota(jnp.int32, (128, 256), 1)
            mask = k <= (r // 64) * 128 + c * 64 + r % 64
            keys = pl.ds(base + tile * 256, 256)
            absorb(q, pairs[keys, :HD], pairs[keys, HD:], peak, total, accum, rows, mask)
            if tile:
                keys = pl.ds(base, tile * 256)
                absorb(q, pairs[keys, :HD], pairs[keys, HD:], peak, total, accum, rows)
    for tile in range(2):
        rows = pl.ds(512 + tile * 256, 256)
        keys = pl.ds(0, 1024)
        absorb(query[rows, :], pairs[keys, :HD], pairs[keys, HD:], peak, total, accum, rows)


def own_attention(query, pairs):
    shape = jax.ShapeDtypeStruct((1024, HD), F32)
    return pl.pallas_call(
        own_kernel,
        out_shape=(shape,) * 3,
        in_specs=[VMEM_SPEC] * 2,
        out_specs=(VMEM_SPEC,) * 3,
        compiler_params=params(),
        name="attend_own",
    )(query, pairs)


def absorb_plane(query, low, high, plane, y, peak, total, accum):
    def run(block, source):
        for tile in range(2):
            rows = pl.ds(block * 512 + tile * 256, 256)
            absorb(query[rows, :], source[:, :HD], source[:, HD:], peak, total, accum, rows)

    run(1, low)

    @pl.when(plane < y)
    def _():
        run(0, low)
        run(1, high)


def near_kernel(query, behind0, behind1, ahead0, ahead1, peak_in, total_in, accum_in,
                peak, total, accum, buffer, sems):
    x, y, z, c = place()
    copies = []
    for i, (mine, partner) in enumerate(((behind0, behind1), (ahead0, ahead1))):
        copies.append(pltpu.make_async_copy(mine, buffer.at[i, c], sems.at[i, 0]))
        copies.append(pltpu.make_async_copy(partner, buffer.at[i, 1 - c], sems.at[i, 1]))
    for copy in copies:
        copy.start()
    peak[...] = peak_in[...]
    total[...] = total_in[...]
    accum[...] = accum_in[...]
    for i in range(2):
        copies[2 * i].wait()
        copies[2 * i + 1].wait()
        plane = (y + 3) % 4 if i == 0 else (y + 1) % 4
        absorb_plane(query, buffer.at[i, 0], buffer.at[i, 1], plane, y, peak, total, accum)


def near_attention(query, behind, ahead, state):
    shape = jax.ShapeDtypeStruct((1024, HD), F32)
    return pl.pallas_call(
        near_kernel,
        out_shape=(shape,) * 3,
        in_specs=[VMEM_SPEC] + [ANY_SPEC] * 4 + [VMEM_SPEC] * 3,
        out_specs=(VMEM_SPEC,) * 3,
        scratch_shapes=[
            pltpu.VMEM((2, 2, 1024, 2 * HD), BF16),
            pltpu.SemaphoreType.DMA((2, 2)),
        ],
        compiler_params=params(),
        name="attend_near",
    )(query, *behind, *ahead, *state)


def far_kernel(query, head0, tail0, head1, tail1, peak_in, total_in, accum_in,
               out0, out1, out2, out3, peak, total, accum, buffer, sems):
    x, y, z, c = place()
    copies = [
        pltpu.make_async_copy(head0, buffer.at[c, 0:512], sems.at[0]),
        pltpu.make_async_copy(tail0, buffer.at[c, 512:1024], sems.at[1]),
        pltpu.make_async_copy(head1, buffer.at[1 - c, 0:512], sems.at[2]),
        pltpu.make_async_copy(tail1, buffer.at[1 - c, 512:1024], sems.at[3]),
    ]
    for copy in copies:
        copy.start()
    peak[...] = peak_in[...]
    total[...] = total_in[...]
    accum[...] = accum_in[...]
    for copy in copies:
        copy.wait()
    absorb_plane(query, buffer.at[0], buffer.at[1], (y + 2) % 4, y, peak, total, accum)
    accum[...] = accum[...] / total[...]
    for d, out in enumerate((out0, out1, out2, out3)):
        oz = (z + d) % 4
        for ox in range(4):
            row = pl.multiple_of((ox % 2) * 512 + (oz * 2 + ox // 2) * 64, 64)
            out[ox * 64:(ox + 1) * 64, :] = accum[pl.ds(row, 64), :].astype(BF16)


def far_attention(query, pieces, state):
    return pl.pallas_call(
        far_kernel,
        out_shape=(jax.ShapeDtypeStruct((256, HD), BF16),) * 4,
        in_specs=[VMEM_SPEC] + [ANY_SPEC] * 4 + [VMEM_SPEC] * 3,
        out_specs=(VMEM_SPEC,) * 4,
        scratch_shapes=[
            pltpu.VMEM((1024, HD), F32),
            pltpu.VMEM((1024, HD), F32),
            pltpu.VMEM((1024, HD), F32),
            pltpu.VMEM((2, 1024, 2 * HD), BF16),
            pltpu.SemaphoreType.DMA((4,)),
        ],
        compiler_params=params(),
        name="attend_far",
    )(query, *pieces, *state)


def project_kernel(*refs):
    pieces, own, other = refs[0:4], refs[4:8], refs[8:12]
    outs, weight, sums, sems = refs[12:16], refs[16], refs[17], refs[18]
    x, y, z, c = place()
    copies = []
    for d in range(4):
        for r in range(2):
            for side in range(2):
                core = c if side == 0 else 1 - c
                column = 2 * ((x // 2 + r) % 2) + core
                source = own[d] if side == 0 else other[d]
                copies.append(pltpu.make_async_copy(
                    source.at[r], weight.at[column, d * HD:(d + 1) * HD], sems.at[d, r, side]))
    for copy in copies:
        copy.start()
    for copy in copies:
        copy.wait()
    acc = None
    for e in range(4):
        part = dot(pieces[e][...], weight[(x + e) % 4])
        acc = part if acc is None else acc + part
    sums[...] = acc
    for e in range(4):
        row = pl.multiple_of(((x + e) % 4) * 64, 64)
        outs[e][...] = sums[pl.ds(row, 64), :].astype(BF16)


def project(pieces, own, other):
    return pl.pallas_call(
        project_kernel,
        out_shape=(jax.ShapeDtypeStruct((64, 1024), BF16),) * 4,
        in_specs=[VMEM_SPEC] * 4 + [ANY_SPEC] * 8,
        out_specs=(VMEM_SPEC,) * 4,
        scratch_shapes=[
            pltpu.VMEM((4, 512, 1024), BF16),
            pltpu.VMEM((256, 1024), F32),
            pltpu.SemaphoreType.DMA((4, 2, 2)),
        ],
        compiler_params=params(),
        name="project",
    )(*pieces, *own, *other)


def finish_kernel(frames, p0, p1, p2, p3, out):
    x = place()[0]
    for e, piece in enumerate((p0, p1, p2, p3)):
        column = pl.multiple_of(((x + 4 - e) % 4) * 1024, 1024)
        cols = pl.ds(column, 1024)
        out[:, cols] = (frames[:, cols].astype(F32) + piece[...].astype(F32)).astype(BF16)


def finish(frames, pieces):
    return pl.pallas_call(
        finish_kernel,
        out_shape=jax.ShapeDtypeStruct(frames.shape, BF16),
        in_specs=[VMEM_SPEC] * 5,
        out_specs=VMEM_SPEC,
        compiler_params=params(),
        name="finish",
    )(frames, *pieces)


def body(
    audio_feats, conv_first, conv_second, down_weight, in_proj, norm_gain, qkv_weight, out_weight
):
    rows = audio_feats.shape[0]
    halo = lax.ppermute(audio_feats[rows - HALO:], AXES, [(i, i + 1) for i in range(127)])
    x = place()[0]

    chunk = out_weight.shape[1] // 4
    keep = lax.dynamic_slice_in_dim(out_weight, x * chunk, chunk, 1)
    give = lax.dynamic_slice_in_dim(out_weight, (3 - x) * chunk, chunk, 1)
    got = send(give, lambda x, y, z, c: (3 - x, y, z, c))
    columns = jnp.stack([keep, got], axis=0)

    frames, latent = encode_frames(
        halo, audio_feats, conv_first, conv_second, down_weight, in_proj)

    near = jnp.concatenate(
        [latent] + [from_first(latent, d) for d in (1, 2, 3)], axis=0)
    mine = [near] + [from_second(near, d) for d in (1, 2, 3)]
    partner = [swap_core(piece) for piece in mine]
    composed = compose(in_proj, norm_gain, qkv_weight)
    query, pairs, block = make_qkv(mine + partner, composed, swap_core(composed))

    block, columns = lax.optimization_barrier((block, columns))
    behind = from_y(block, -1)
    ahead = from_y(block, 1)
    behind_pair = (behind, swap_core(behind))
    ahead_pair = (ahead, swap_core(ahead))
    far_head = from_y(behind[:512], -1)
    far_tail = from_y(ahead[512:], 1)

    own_columns = [columns] + [from_z(columns, -d) for d in (1, 2, 3)]
    other_columns = [swap_core(piece) for piece in own_columns]

    state = own_attention(query, pairs)
    state = near_attention(query, behind_pair, ahead_pair, state)
    far = (far_head, far_tail, swap_core(far_head), swap_core(far_tail))
    outs = far_attention(query, far, state)

    heads = [outs[0]] + [from_z(outs[d], -d) for d in (1, 2, 3)]
    wide = jnp.concatenate(heads, axis=1)
    gathered = [wide] + [from_x(wide, e) for e in (1, 2, 3)]
    parts = project(gathered, own_columns, other_columns)
    parts = [parts[0]] + [from_x(parts[e], -e) for e in (1, 2, 3)]
    return finish(frames, parts)


def solution(mesh):
    placed = (P(("seq", "mp"), None), P(), P(), P(), P(), P(), P(None, None, "mp"), P("mp", None))
    return jax.shard_map(
        body, mesh=mesh, in_specs=placed, out_specs=P(("seq", "mp"), None), check_vma=False
    )
```
